128 devices in a mesh: row: 16 (over x, y), col: 8 (over z, core).
Axes of the slice: x: 4, y: 4, z: 4, core: 2. Of those that a mesh axis runs over, the one named last changes fastest.
Arguments:
- diag_tile: float32 [256, 256], replicated, may hold values from 0 to 10, as said below
- panel_block: float32 [24576, 256], P(('row', 'col')), may hold values from -3 to 3
- trailing: bfloat16 [24576, 24576], P('row', 'col'), may hold values from -6 to 6
- vec_head: float32 [512, 256], P('col'), may hold values from -6 to 6
- vec_rest: float32 [512, 24576], P('col', 'row'), may hold values from -6 to 6
Outputs:
- panel: float32 [24576, 256], P(('row', 'col'))
- trailing_new: bfloat16 [24576, 24576], P('row', 'col')
- whitened: float32 [512, 256], P('col')
- vec_new: float32 [512, 24576], P('col', 'row')
The draws below stay inside these ranges and needn't reach their ends.
Inputs may be any that keep to these rules, and one draw needn't show every extreme that they name: `diag_tile`: symmetric positive definite.
All inputs are finite; a program needn't handle non-finite values.
Results may differ from the reference program's by a relative error of at most 0.0054.
Values may be sent and summed in bfloat16 or wider, within the bound.
A program may use at most 128 MiB of HBM per device.

```python
import jax
import jax.numpy as jnp
from jax import lax

NB = 256
NVEC = 512
MR = 24576


def draw_diag_tile(key, part):
    sites = jax.random.uniform(jax.random.fold_in(key, 11), (NB, 2), jnp.float32)
    delta_x = sites[:, 0][:, None] - sites[:, 0][None, :]
    delta_y = sites[:, 1][:, None] - sites[:, 1][None, :]
    distance = jnp.sqrt(delta_x * delta_x + delta_y * delta_y)
    length_scale = 0.3
    kernel = jnp.exp(-distance / length_scale)
    base = kernel + 1.5 * jnp.eye(NB, dtype=jnp.float32)
    return base


def level_of(key, shape, shards, smallest, top_value):
    def one(axis_at, parts):
        steps = jax.random.uniform(jax.random.fold_in(jax.random.fold_in(key, 6), axis_at), (parts,), jnp.float32, smallest / len(shards), top_value / len(shards))
        return jnp.repeat(jnp.exp(steps), shape[axis_at] // parts).reshape((-1,) + (1,) * (len(shape) - axis_at - 1))

    factor_of = one(*shards[0])
    for cut in shards[1:]:
        factor_of = factor_of * one(*cut)
    return factor_of


def bell_draw(own_key, extent, deviation, limit, pieces=(), held_as=jnp.bfloat16):
    values = jax.random.normal(own_key, extent, jnp.float32) * deviation
    if len(pieces) > 0:
        values = level_of(own_key, extent, pieces, -0.22, 0.18) * values
    return jnp.clip(values, min=-limit, max=limit).astype(held_as)


def setup_inputs(seed: int = 0) -> dict:
    key_of = jax.random.split(jax.random.key(seed), 6)
    diag_tile = draw_diag_tile(jax.random.fold_in(key_of[5], 71), 0)
    panel_block = bell_draw(key_of[1], (MR, NB), 0.5, 3.0, ((0, 128),), jnp.float32)
    trailing = bell_draw(key_of[2], (MR, MR), 1.0, 6.0, ((0, 16), (1, 8)))
    vec_head = bell_draw(key_of[3], (NVEC, NB), 1.0, 6.0, ((0, 8),), jnp.float32)
    vec_rest = bell_draw(key_of[4], (NVEC, MR), 1.0, 6.0, ((0, 8), (1, 16)), jnp.float32)
    return dict(diag_tile=diag_tile, panel_block=panel_block, trailing=trailing, vec_head=vec_head, vec_rest=vec_rest)


def right_solve(factor, rhs):
    return lax.linalg.triangular_solve(factor, rhs, left_side=False, lower=True, transpose_a=True)

def reference(diag_tile, panel_block, trailing, vec_head, vec_rest):
    factor = jnp.linalg.cholesky(diag_tile)
    panel = right_solve(factor, panel_block)
    panel_half = panel.astype(jnp.bfloat16)
    blocks = trailing.reshape(MR // NB, NB, MR)
    rows_half = panel_half.reshape(MR // NB, NB, NB)

    def update(pair):
        block, rows = pair
        prod = lax.dot_general(rows.astype(jnp.float32), panel_half.astype(jnp.float32), (((1,), (1,)), ((), ())), preferred_element_type=jnp.float32)
        return (block.astype(jnp.float32) - prod).astype(jnp.bfloat16)
    trailing_new = lax.map(update, (blocks, rows_half)).reshape(MR, MR)
    whitened = right_solve(factor, vec_head)
    whitened_half = whitened.astype(jnp.bfloat16)
    prod = lax.dot_general(whitened_half.astype(jnp.float32), panel_half.astype(jnp.float32), (((1,), (1,)), ((), ())), preferred_element_type=jnp.float32)
    vec_new = vec_rest - prod
    return (panel, trailing_new, whitened, vec_new)
```

```python
import jax
import jax.numpy as jnp
from jax import lax
from jax.experimental import pallas as pl
from jax.experimental.pallas import tpu as pltpu
from jax.sharding import PartitionSpec as P

f32, bf16 = jnp.float32, jnp.bfloat16
MESH = pl.DeviceIdType.MESH
BK = 16
NB = 256
RB = 192
MIB = 1 << 20


def split3(x):
    h = x.astype(bf16)
    r = x - h.astype(f32)
    m = r.astype(bf16)
    return h, m, (r - m.astype(f32)).astype(bf16)


def dot(a, b):
    return lax.dot_general(a, b, (((1,), (0,)), ((), ())), preferred_element_type=f32)


def dot_nt(a, b):
    return lax.dot_general(a, b, (((1,), (1,)), ((), ())), preferred_element_type=f32)


def block_step(k, m_ref, w_ref, g_ref, rhs_ref):
    t, o = divmod(k, 128)
    lane = lax.broadcasted_iota(jnp.int32, (8, 128), 1)
    rows, S = [], []
    for i in range(BK):
        parts = [
            jnp.broadcast_to(m_ref[k + i : k + i + 1, c * 128 : c * 128 + 128], (8, 128)) for c in range(2)
        ]
        S.append([jnp.broadcast_to(parts[t][:, o + j : o + j + 1], (8, 128)) for j in range(i + 1)])
        eye = jnp.where(lane == o + i, 1.0, 0.0)
        parts[t] = jnp.where((lane >= o) & (lane < o + BK), eye, parts[t])
        rows.append(parts)
    inv, F = [], [[None] * BK for _ in range(BK)]
    for j in range(BK):
        inv.append(1.0 / S[j][j])
        for i in range(j + 1, BK):
            F[i][j] = S[i][j] * inv[j]
            for n in range(j + 1, i + 1):
                S[i][n] = S[i][n] - F[i][j] * S[n][j]
            rows[i] = [rows[i][c] - F[i][j] * rows[j][c] for c in range(2)]
    for i in range(BK):
        rs = lax.rsqrt(S[i][i])
        for c in range(2):
            v = rows[i][c] * rs
            if c == t:
                v = jnp.where(lane < o + BK, v, 0.0)
            elif c > t:
                v = jnp.zeros_like(v)
            w_ref[k + i : k + i + 1, c * 128 : c * 128 + 128] = v[0:1]
    if k + BK >= NB:
        return
    g = [None] * BK
    for i in reversed(range(BK)):
        acc = [rows[i][c] * inv[i] for c in range(2)]
        for j in range(i + 1, BK):
            acc = [acc[c] - F[j][i] * g[j][c] for c in range(2)]
        g[i] = acc
        for c in range(2):
            g_ref[i : i + 1, c * 128 : c * 128 + 128] = acc[c][0:1]
    gh, gm, gl = split3(g_ref[...])
    for q, (a, b) in enumerate(((gh, gh), (gm, gm), (gl, gh))):
        rhs_ref[q, o : o + BK, :] = a
        rhs_ref[q, 128 + o : 128 + o + BK, :] = b
    n0 = k + BK
    h, m, l = split3(m_ref[n0:NB, t * 128 : t * 128 + 128])
    hm = jnp.concatenate([h, m], 1)
    up = dot(hm, rhs_ref[0]) + dot(hm, rhs_ref[1])
    up = up + dot(jnp.concatenate([h, l], 1), rhs_ref[2])
    lanes = lax.broadcasted_iota(jnp.int32, (NB - n0, NB), 1)
    old = jnp.where((lanes >= k) & (lanes < k + BK), 0.0, m_ref[n0:NB, :])
    m_ref[n0:NB, :] = old - up
    zero = jnp.zeros((BK, NB), bf16)
    for q in range(3):
        rhs_ref[q, o : o + BK, :] = zero
        rhs_ref[q, 128 + o : 128 + o + BK, :] = zero


def factor_kernel(a_ref, b_ref, v_ref, panel_ref, white_ref, xh_ref, wh_ref, m_ref, w_ref, g_ref, rhs_ref):
    m_ref[...] = a_ref[...]
    rhs_ref[...] = jnp.zeros_like(rhs_ref)
    for k in range(0, NB, BK):
        block_step(k, m_ref, w_ref, g_ref, rhs_ref)
    wh, wm, _ = split3(w_ref[...])

    def solve(x):
        h, m, _ = split3(x)
        return dot_nt(h, wh) + (dot_nt(h, wm) + dot_nt(m, wh))

    x = solve(b_ref[...])
    panel_ref[...] = x
    half = x.astype(bf16)
    xh_ref[0] = half[:, 0:128]
    xh_ref[1] = half[:, 128:256]
    v = solve(v_ref[...])
    white_ref[...] = v
    wh_ref[...] = v.astype(bf16)


class Torus:
    def __init__(self):
        row, col = lax.axis_index("row"), lax.axis_index("col")
        self.x, self.y = row // 4, row % 4
        self.z, self.c = col // 2, col % 2

    def at(self, x=None, y=None, z=None, c=None):
        x = self.x if x is None else x
        y = self.y if y is None else y
        z = self.z if z is None else z
        c = self.c if c is None else c
        return {"row": x * 4 + y, "col": z * 2 + c}

    def step(self, dim, by):
        return self.at(**{dim: (getattr(self, dim) + by) % 4})

    def held(self, hx, hy):
        same = jnp.where(hy // 2 == self.c, 1, 0)
        yy = jnp.where(same == 1, hy, 3 - hy)
        return (yy % 2) * 8 + 2 * hx + (1 - same)


def comm_kernel(x_ref, row_ref, col_ref, send, recv, local):
    me = Torus()
    barrier = pltpu.get_barrier_semaphore()
    same = jnp.where(me.y // 2 == me.c, 1, 0)
    src = (me.z, jnp.where(same == 1, me.y, 3 - me.y), me.x, 1 - same)
    dst = (me.z, jnp.where(me.c == 0, me.y, 3 - me.y), me.x, me.y // 2)
    own = (dst[0] == me.x) & (dst[1] == me.y) & (dst[2] == me.z) & (dst[3] == me.c)
    away = jnp.logical_not(own)
    for dim in ("x", "y", "z"):
        for by in (1, -1):
            pl.semaphore_signal(barrier, inc=1, device_id=me.step(dim, by), device_id_type=MESH)
    pl.semaphore_signal(barrier, inc=1, device_id=me.at(c=1 - me.c), device_id_type=MESH)

    @pl.when(away)
    def _():
        pl.semaphore_signal(barrier, inc=1, device_id=me.at(*src), device_id_type=MESH)
        pl.semaphore_wait(barrier, 8)

    @pl.when(own)
    def _():
        pl.semaphore_wait(barrier, 7)

    started = []

    def copy(a, b, idx, to):
        return pltpu.make_async_remote_copy(
            src_ref=a, dst_ref=b, send_sem=send.at[idx], recv_sem=recv.at[idx], device_id=to, device_id_type=MESH
        )

    def go(a, b, idx, to):
        d = copy(a, b, idx, to)
        d.start()
        started.append(d)

    def rows_of(ref, block, lo, n):
        return ref.at[:, pl.ds(pl.multiple_of(block * RB + lo, 16), n), :]

    def wait(ref, idx):
        copy(ref, ref, idx, me.at(c=1 - me.c)).wait_recv()

    first = me.at(*dst)
    mine = (me.y % 2) * 8 + 2 * me.z + me.c
    hold = me.held(me.x, me.y)
    sc = copy(x_ref, rows_of(col_ref, mine, 0, RB), 0, first)

    @pl.when(away)
    def _():
        sc.start()

    @pl.when(own)
    def _():
        pltpu.make_async_copy(x_ref, rows_of(col_ref, hold, 0, RB), recv.at[0]).start()

    zb = lambda d, core=None: 2 * ((me.z + d) % 4) + (me.c if core is None else core)
    sib = me.at(c=1 - me.c)
    keep = pltpu.make_async_copy(x_ref, rows_of(row_ref, zb(0), 0, RB), local)
    keep.start()
    go(x_ref, rows_of(row_ref, zb(0), 0, RB), 1, me.step("z", 1))
    go(x_ref, rows_of(row_ref, zb(0), 0, RB), 2, me.step("z", -1))
    go(x_ref, rows_of(row_ref, zb(0), 0, RB), 5, sib)

    H, Q = RB // 2, RB // 4
    parts = ((0, "x", "y", 9), (H, "y", "x", 29))

    def chunk(part, a, b, lo=0, n=H):
        base, d1, d2, _ = part
        p = (getattr(me, d1) + a) % 4
        q = (getattr(me, d2) + b) % 4
        hx, hy = (p, q) if d1 == "x" else (q, p)
        return rows_of(col_ref, me.held(hx, hy), base + lo, n)

    REL = (0, -1, 1, 2)

    def send2(part, rel, lo=0, n=H):
        _, d1, d2, sem = part
        ref = chunk(part, REL[rel], 0, lo, n)
        go(ref, ref, sem + 4 + 4 * rel + 0, me.step(d2, 1))
        go(ref, ref, sem + 4 + 4 * rel + 1, me.step(d2, -1))

    def forward(part, dim, sem, ref_lo, ref_hi, which):
        if which == 0:
            go(ref_lo, ref_lo, sem + 2, me.step(dim, 1))
        else:
            go(ref_hi, ref_hi, sem + 3, me.step(dim, -1))

    def dim1(part, which):
        _, d1, d2, sem = part
        a = (-1, 1)[which]
        wait(chunk(part, a, 0), sem + which)
        forward(part, d1, sem, chunk(part, a, 0, 0, Q), chunk(part, a, 0, Q, Q), which)
        send2(part, 1 + which)

    def dim2(part, rel, which):
        _, d1, d2, sem = part
        b = (-1, 1)[which]
        s = sem + 4 + 4 * rel
        wait(chunk(part, REL[rel], b), s + which)
        forward(part, d2, s, chunk(part, REL[rel], b, 0, Q), chunk(part, REL[rel], b, Q, Q), which)

    def far1(part):
        sem = part[3]
        wait(chunk(part, 2, 0, 0, Q), sem + 2)
        wait(chunk(part, 2, 0, Q, Q), sem + 3)
        send2(part, 3)

    def far2(part, rel):
        s = part[3] + 4 + 4 * rel
        wait(chunk(part, REL[rel], 2, 0, Q), s + 2)
        wait(chunk(part, REL[rel], 2, Q, Q), s + 3)

    wait(rows_of(col_ref, hold, 0, RB), 0)
    for part in parts:
        ref, sem = chunk(part, 0, 0), part[3]
        go(ref, ref, sem + 0, me.step(part[1], 1))
        go(ref, ref, sem + 1, me.step(part[1], -1))
    for part in parts:
        send2(part, 0)
    for w in range(2):
        d = (-1, 1)[w]
        blk = zb(d)
        wait(rows_of(row_ref, blk, 0, RB), 1 + w)
        half = rows_of(row_ref, blk, w * H, H)
        go(half, half, 3 + w, me.step("z", (1, -1)[w]))
        whole = rows_of(row_ref, blk, 0, RB)
        go(whole, whole, 6 + w, sib)
    for w in range(2):
        for part in parts:
            dim1(part, w)
    for w in range(2):
        for part in parts:
            dim2(part, 0, w)
    for part in parts:
        far1(part)
    for w in range(2):
        wait(rows_of(row_ref, zb(2), w * H, H), 3 + w)
    whole = rows_of(row_ref, zb(2), 0, RB)
    go(whole, whole, 8, sib)
    for rel in (1, 2, 3):
        for w in range(2):
            for part in parts:
                dim2(part, rel, w)
    for rel in range(4):
        for part in parts:
            far2(part, rel)
    for i, d in enumerate((0, -1, 1, 2)):
        wait(rows_of(row_ref, zb(d, 1 - me.c), 0, RB), 5 + i)
    keep.wait()
    for d in started:
        d.wait_send()

    @pl.when(away)
    def _():
        sc.wait_send()


def update_kernel(row_ref, col_ref, t_ref, wh_ref, v_ref, out_ref, vec_ref):
    i, j = pl.program_id(0), pl.program_id(1)
    tm, tn = out_ref.shape
    r = jnp.concatenate([row_ref[0, pl.ds(i * tm, tm), :], row_ref[1, pl.ds(i * tm, tm), :]], 1)
    c = jnp.concatenate([col_ref[0, pl.ds(j * tn, tn), :], col_ref[1, pl.ds(j * tn, tn), :]], 1)
    out_ref[...] = (t_ref[...].astype(f32) - dot_nt(r, c)).astype(bf16)

    @pl.when((i == 0) & (j == 0))
    def _():
        full = jnp.concatenate([row_ref[0], row_ref[1]], 1)
        vec_ref[...] = v_ref[...] - dot_nt(wh_ref[...], full)


VM = pl.BlockSpec(memory_space=pltpu.VMEM)


def per_device(diag_tile, panel_block, trailing, vec_head, vec_rest):
    nv = vec_head.shape[0]
    mr, mc = trailing.shape
    panel, white, xh, wh = pl.pallas_call(
        factor_kernel,
        out_shape=(
            jax.ShapeDtypeStruct((RB, NB), f32),
            jax.ShapeDtypeStruct((nv, NB), f32),
            jax.ShapeDtypeStruct((2, RB, 128), bf16),
            jax.ShapeDtypeStruct((nv, NB), bf16),
        ),
        in_specs=[VM] * 3,
        out_specs=(VM,) * 4,
        scratch_shapes=[
            pltpu.VMEM((NB, NB), f32),
            pltpu.VMEM((NB, NB), f32),
            pltpu.VMEM((BK, NB), f32),
            pltpu.VMEM((3, NB, NB), bf16),
        ],
        compiler_params=pltpu.CompilerParams(vmem_limit_bytes=12 * MIB),
        cost_estimate=pl.CostEstimate(flops=12 * 10**9, bytes_accessed=0, transcendentals=0),
        name="factor",
    )(diag_tile, panel_block, vec_head)
    rowp, colp = pl.pallas_call(
        comm_kernel,
        out_shape=(jax.ShapeDtypeStruct((2, mr, 128), bf16), jax.ShapeDtypeStruct((2, mc, 128), bf16)),
        in_specs=[VM],
        out_specs=(VM,) * 2,
        scratch_shapes=[
            pltpu.SemaphoreType.DMA((49,)),
            pltpu.SemaphoreType.DMA((49,)),
            pltpu.SemaphoreType.DMA,
        ],
        compiler_params=pltpu.CompilerParams(
            collective_id=0, has_side_effects=True, vmem_limit_bytes=12 * MIB
        ),
        cost_estimate=pl.CostEstimate(flops=10 * 10**9, bytes_accessed=0, transcendentals=0),
        name="share",
    )(xh)
    tm, tn = 512, 1024
    out, vec = pl.pallas_call(
        update_kernel,
        grid=(mr // tm, mc // tn),
        out_shape=(jax.ShapeDtypeStruct((mr, mc), bf16), jax.ShapeDtypeStruct((nv, mr), f32)),
        in_specs=[
            VM,
            VM,
            pl.BlockSpec((tm, tn), lambda i, j: (i, j)),
            VM,
            VM,
        ],
        out_specs=(pl.BlockSpec((tm, tn), lambda i, j: (i, j)), pl.BlockSpec((nv, mr), lambda i, j: (0, 0))),
        compiler_params=pltpu.CompilerParams(vmem_limit_bytes=40 * MIB),
        name="update",
    )(rowp, colp, trailing, wh, vec_rest)
    return (panel, out, white, vec)


def solution(mesh):
    in_specs = (P(), P(("row", "col"), None), P("row", "col"), P("col", None), P("col", "row"))
    out_specs = (P(("row", "col"), None), P("row", "col"), P("col", None), P("col", "row"))
    return jax.shard_map(per_device, mesh=mesh, in_specs=in_specs, out_specs=out_specs, check_vma=False)
```

```python
import jax
import jax.numpy as jnp
from jax import lax
from jax.experimental import pallas as pl
from jax.experimental.pallas import tpu as pltpu
from jax.sharding import PartitionSpec as P

f32, bf16 = jnp.float32, jnp.bfloat16
MESH = pl.DeviceIdType.MESH
BK = 16
NB = 256
RB = 192
MIB = 1 << 20


def split3(x):
    h = x.astype(bf16)
    r = x - h.astype(f32)
    m = r.astype(bf16)
    return h, m, (r - m.astype(f32)).astype(bf16)


def dot(a, b):
    return lax.dot_general(a, b, (((1,), (0,)), ((), ())), preferred_element_type=f32)


def dot_nt(a, b):
    return lax.dot_general(a, b, (((1,), (1,)), ((), ())), preferred_element_type=f32)


def block_step(k, m_ref, w_ref, g_ref, rhs_ref):
    t, o = divmod(k, 128)
    lane = lax.broadcasted_iota(jnp.int32, (1, 8, 128), 2)
    nth = lax.broadcasted_iota(jnp.int32, (BK, 8, 128), 0)
    R = [
        jnp.stack([jnp.broadcast_to(m_ref[k + i : k + i + 1, c * 128 : c * 128 + 128], (8, 128)) for i in range(BK)])
        for c in range(2)
    ]
    S = [jnp.broadcast_to(R[t][j:, :, o + j : o + j + 1], (BK - j, 8, 128)) for j in range(BK)]
    R[t] = jnp.where((lane >= o) & (lane < o + BK), jnp.where(lane - o == nth, 1.0, 0.0), R[t])
    inv, F, out = [], [], [[], []]
    for j in range(BK):
        inv.append(1.0 / S[j][0:1])
        for c in range(2):
            out[c].append(R[c][0:1])
        if j == BK - 1:
            break
        f = S[j][1:] * inv[j]
        for n in range(j + 1, BK):
            S[n] = S[n] - f[n - j - 1 :] * S[j][n - j : n - j + 1]
        R = [R[c][1:] - f * R[c][0:1] for c in range(2)]
        F.append(f)
    piv = jnp.concatenate([S[j][0:1] for j in range(BK)], 0)
    rs = lax.rsqrt(piv)
    U = [jnp.concatenate(out[c], 0) for c in range(2)]
    for c in range(2):
        v = U[c] * rs
        if c == t:
            v = jnp.where(lane < o + BK, v, 0.0)
        elif c > t:
            v = jnp.zeros_like(v)
        for i in range(BK):
            w_ref[k + i : k + i + 1, c * 128 : c * 128 + 128] = v[i, 0:1]
    if k + BK >= NB:
        return
    iv = jnp.concatenate(inv, 0)
    Z = [U[c] * iv for c in range(2)]
    for i in reversed(range(BK)):
        for c in range(2):
            g_ref[i : i + 1, c * 128 : c * 128 + 128] = Z[c][i, 0:1]
        if i:
            f = jnp.concatenate([F[n][i - n - 1 : i - n] for n in range(i)], 0)
            Z = [Z[c][:i] - f * Z[c][i : i + 1] for c in range(2)]
    gh, gm, gl = split3(g_ref[...])
    for q, (a, b) in enumerate(((gh, gh), (gm, gm), (gl, gh))):
        rhs_ref[q, o : o + BK, :] = a
        rhs_ref[q, 128 + o : 128 + o + BK, :] = b
    n0 = k + BK
    h, m, l = split3(m_ref[n0:NB, t * 128 : t * 128 + 128])
    hm = jnp.concatenate([h, m], 1)
    up = dot(hm, rhs_ref[0]) + dot(hm, rhs_ref[1])
    up = up + dot(jnp.concatenate([h, l], 1), rhs_ref[2])
    lanes = lax.broadcasted_iota(jnp.int32, (NB - n0, NB), 1)
    old = jnp.where((lanes >= k) & (lanes < k + BK), 0.0, m_ref[n0:NB, :])
    m_ref[n0:NB, :] = old - up
    zero = jnp.zeros((BK, NB), bf16)
    for q in range(3):
        rhs_ref[q, o : o + BK, :] = zero
        rhs_ref[q, 128 + o : 128 + o + BK, :] = zero


class Torus:
    def __init__(self):
        row, col = lax.axis_index("row"), lax.axis_index("col")
        self.x, self.y = row // 4, row % 4
        self.z, self.c = col // 2, col % 2

    def at(self, x=None, y=None, z=None, c=None):
        x = self.x if x is None else x
        y = self.y if y is None else y
        z = self.z if z is None else z
        c = self.c if c is None else c
        return {"row": x * 4 + y, "col": z * 2 + c}

    def step(self, dim, by):
        return self.at(**{dim: (getattr(self, dim) + by) % 4})


NSEM = 22


class Share:
    def __init__(self, me, half, x_ref, row_ref, col_ref, send, recv):
        self.me, self.half = me, half
        self.x, self.row, self.col = x_ref.at[half], row_ref.at[half], col_ref.at[half]
        self.send, self.recv = send.at[half], recv.at[half]
        self.started = []

    def copy(self, a, b, sem, to, arrive=None):
        return pltpu.make_async_remote_copy(
            src_ref=a,
            dst_ref=b,
            send_sem=self.send.at[sem],
            recv_sem=self.recv.at[sem if arrive is None else arrive],
            device_id=to,
            device_id_type=MESH,
        )

    def origin(self, y):
        same = jnp.where(y // 2 == self.me.c, 1, 0)
        return jnp.where(same == 1, y, 3 - y) % 2, 1 - same

    def scatter(self):
        me = self.me
        yh = jnp.where(me.c == 0, me.y, 3 - me.y)
        for part in range(2):
            src = self.x.at[part]
            dst = self.col.at[me.y % 2, me.z, me.c, part]
            arrive = part
            for d in range(4):
                if part == 0:
                    to = me.at((me.x + d) % 4, yh, me.x, me.y // 2)
                else:
                    to = me.at(me.z, (me.y + d) % 4, me.x, me.y // 2)
                cp = self.copy(src, dst, 4 * part + d, to, arrive)
                if d == 0:
                    mine = me.own[part]

                    @pl.when(jnp.logical_not(mine))
                    def _():
                        cp.start()

                    @pl.when(mine)
                    def _():
                        pltpu.make_async_copy(src, dst, self.recv.at[arrive]).start()
                else:
                    cp.start()
                self.started.append((cp, me.own[part] if d == 0 else None))

    def rows(self):
        me = self.me
        dst = self.row.at[2 * me.z + me.c]
        i = 0
        for d in range(4):
            for e in range(2):
                if d == 0 and e == 0:
                    continue
                cp = self.copy(self.x, dst, 8 + i, me.at(z=(me.z + d) % 4, c=(me.c + e) % 2))
                cp.start()
                self.started.append((cp, None))
                i += 1
        self.keep = pltpu.make_async_copy(self.x, dst, self.send.at[21])
        self.keep.start()

    def held(self, part, at):
        if part == 0:
            yy, cc = self.origin(at)
            return self.col.at[yy, :, cc, 0]
        return self.col.at[:, at, :, 1]

    def relay(self):
        me = self.me
        for part in range(2):
            dim = "yx"[part]
            ref = self.held(part, getattr(me, dim))
            self.copy(ref, ref, part, me.step(dim, 1), part).wait_recv()
            for d in range(1, 4):
                cp = self.copy(ref, ref, 15 + 3 * part + d - 1, me.step(dim, d))
                cp.start()
                self.started.append((cp, None))

    def finish(self):
        me = self.me
        i = 0
        for d in range(4):
            for e in range(2):
                if d == 0 and e == 0:
                    continue
                dst = self.row.at[2 * ((me.z + 4 - d) % 4) + (me.c + e) % 2]
                self.copy(dst, dst, 8 + i, me.step("z", 1)).wait_recv()
                i += 1
        self.keep.wait()
        for part in range(2):
            dim = "yx"[part]
            for d in range(1, 4):
                ref = self.held(part, (getattr(me, dim) + 4 - d) % 4)
                self.copy(ref, ref, 15 + 3 * part + d - 1, me.step(dim, 1)).wait_recv()
        for cp, unless in self.started:
            if unless is None:
                cp.wait_send()
            else:

                @pl.when(jnp.logical_not(unless))
                def _():
                    cp.wait_send()


def greet(me):
    barrier = pltpu.get_barrier_semaphore()

    def tell(to):
        pl.semaphore_signal(barrier, inc=1, device_id=to, device_id_type=MESH)

    same = jnp.where(me.y // 2 == me.c, 1, 0)
    fy = jnp.where(same == 1, me.y, 3 - me.y)
    me.own = (
        (me.x == me.z) & (me.y // 2 == me.c) & (me.c == 0),
        (me.x == me.z) & (me.y // 2 == me.c),
    )
    for d in range(4):
        to = me.at(me.z, fy, (me.z + d) % 4, 1 - same)
        if d == 0:
            pl.when(jnp.logical_not(me.own[0]))(lambda: tell(to))
        else:
            tell(to)
    for d in range(4):
        to = me.at(me.z, 2 * me.c + (me.y + d // 2) % 2, me.x, (me.c + d) % 2)
        if d == 0:
            pl.when(jnp.logical_not(me.own[1]))(lambda: tell(to))
        else:
            tell(to)
    for d in range(4):
        for e in range(2):
            if d or e:
                tell(me.at(z=(me.z + d) % 4, c=(me.c + e) % 2))
    for dim in "xy":
        for d in range(1, 4):
            tell(me.step(dim, d))
    return barrier, 21 - jnp.where(me.own[0], 1, 0) - jnp.where(me.own[1], 1, 0)


def panel_kernel(
    a_hbm, b_hbm, v_hbm, panel_ref, white_ref, wh_ref, row_ref, col_ref,
    m_ref, w_ref, g_ref, rhs_ref, bv_ref, x_ref, send, recv, local,
):
    loads = [
        pltpu.make_async_copy(a_hbm, m_ref, local.at[0]),
        pltpu.make_async_copy(b_hbm, bv_ref.at[0:RB], local.at[1]),
        pltpu.make_async_copy(v_hbm, bv_ref.at[RB:NB], local.at[2]),
    ]
    for cp in loads:
        cp.start()
    me = Torus()
    barrier, count = greet(me)
    rhs_ref[...] = jnp.zeros_like(rhs_ref)
    shares = [Share(me, h, x_ref, row_ref, col_ref, send, recv) for h in range(2)]
    loads[0].wait()
    for k in range(0, NB, BK):
        block_step(k, m_ref, w_ref, g_ref, rhs_ref)
        if k == RELAY_AFTER:
            shares[0].relay()
        if k + BK in (128, 256):
            half = k // 128
            n = k + BK
            if half == 0:
                loads[1].wait()
                loads[2].wait()
            wh, wm, _ = split3(w_ref[half * 128 : n, 0:n])
            bh, bm, _ = split3(bv_ref[:, 0:n])
            x = dot_nt(bh, wh) + (dot_nt(bh, wm) + dot_nt(bm, wh))
            xb = x.astype(bf16)
            for part in range(2):
                x_ref[half, part] = xb[part * 96 : part * 96 + 96]
            panel_ref[:, half * 128 : n] = x[0:RB]
            white_ref[:, half * 128 : n] = x[RB:NB]
            wh_ref[:, half * 128 : n] = xb[RB:NB]
            if half == 0:
                pl.semaphore_wait(barrier, count)
            shares[half].scatter()
            shares[half].rows()
    shares[1].relay()
    for s in shares:
        s.finish()


def update_kernel(row_ref, col_ref, t_ref, wh_ref, v_ref, p_in, w_in, out_ref, vec_ref, p_ref, w_ref):
    i = pl.program_id(0)
    tm = out_ref.shape[0]
    rs = pl.ds(pl.multiple_of(i * tm, tm), tm)
    r = jnp.concatenate([row_ref[0, rs, :], row_ref[1, rs, :]], 1)
    c = jnp.concatenate([col_ref[0], col_ref[1]], 1)
    out_ref[...] = (t_ref[rs, :].astype(f32) - dot_nt(r, c)).astype(bf16)

    @pl.when(i == 0)
    def _():
        full = jnp.concatenate([row_ref[0], row_ref[1]], 1)
        vec_ref[...] = v_ref[...] - dot_nt(wh_ref[...], full)
        p_ref[...] = p_in[...]
        w_ref[...] = w_in[...]


VM = pl.BlockSpec(memory_space=pltpu.VMEM)
HB = pl.BlockSpec(memory_space=pltpu.MemorySpace.HBM)
RELAY_AFTER = 13 * BK


def per_device(diag_tile, panel_block, trailing, vec_head, vec_rest):
    nv = vec_head.shape[0]
    mr, mc = trailing.shape
    panel, white, wh, rowp, colp = pl.pallas_call(
        panel_kernel,
        out_shape=(
            jax.ShapeDtypeStruct((RB, NB), f32),
            jax.ShapeDtypeStruct((nv, NB), f32),
            jax.ShapeDtypeStruct((nv, NB), bf16),
            jax.ShapeDtypeStruct((2, 8, 2, 96, 128), bf16),
            jax.ShapeDtypeStruct((2, 2, 4, 2, 2, 96, 128), bf16),
        ),
        in_specs=[HB] * 3,
        out_specs=(VM,) * 5,
        scratch_shapes=[
            pltpu.VMEM((NB, NB), f32),
            pltpu.VMEM((NB, NB), f32),
            pltpu.VMEM((BK, NB), f32),
            pltpu.VMEM((3, NB, NB), bf16),
            pltpu.VMEM((NB, NB), f32),
            pltpu.VMEM((2, 2, 96, 128), bf16),
            pltpu.SemaphoreType.DMA((2, NSEM)),
            pltpu.SemaphoreType.DMA((2, NSEM)),
            pltpu.SemaphoreType.DMA((3,)),
        ],
        compiler_params=pltpu.CompilerParams(
            collective_id=0, has_side_effects=True, vmem_limit_bytes=12 * MIB
        ),
        cost_estimate=pl.CostEstimate(flops=20 * 10**9, bytes_accessed=0, transcendentals=0),
        name="panel",
    )(diag_tile, panel_block, vec_head)
    rowp = rowp.reshape(2, mr, 128)
    colp = colp.reshape(2, mc, 128)
    tm = 384
    whole = lambda shape: pl.BlockSpec(shape, lambda i: (0, 0))
    out, vec, panel, white = pl.pallas_call(
        update_kernel,
        grid=(mr // tm,),
        out_shape=(
            jax.ShapeDtypeStruct((mr, mc), bf16),
            jax.ShapeDtypeStruct((nv, mr), f32),
            jax.ShapeDtypeStruct((RB, NB), f32),
            jax.ShapeDtypeStruct((nv, NB), f32),
        ),
        in_specs=[VM] * 7,
        out_specs=(
            pl.BlockSpec((tm, mc), lambda i: (i, 0)),
            whole((nv, mr)),
            whole((RB, NB)),
            whole((nv, NB)),
        ),
        compiler_params=pltpu.CompilerParams(vmem_limit_bytes=40 * MIB),
        name="update",
    )(rowp, colp, trailing, wh, vec_rest, panel, white)
    return (panel, out, white, vec)


def solution(mesh):
    in_specs = (P(), P(("row", "col"), None), P("row", "col"), P("col", None), P("col", "row"))
    out_specs = (P(("row", "col"), None), P("row", "col"), P("col", None), P("col", "row"))
    return jax.shard_map(per_device, mesh=mesh, in_specs=in_specs, out_specs=out_specs, check_vma=False)
```

```python
import jax
import jax.numpy as jnp
from jax import lax
from jax.experimental import pallas as pl
from jax.experimental.pallas import tpu as pltpu
from jax.sharding import PartitionSpec as P

f32, bf16 = jnp.float32, jnp.bfloat16
MESH = pl.DeviceIdType.MESH
BK = 16
NB = 256
RB = 192
MIB = 1 << 20


def split3(x):
    h = x.astype(bf16)
    r = x - h.astype(f32)
    m = r.astype(bf16)
    return h, m, (r - m.astype(f32)).astype(bf16)


def dot(a, b):
    return lax.dot_general(a, b, (((1,), (0,)), ((), ())), preferred_element_type=f32)


def dot_nt(a, b):
    return lax.dot_general(a, b, (((1,), (1,)), ((), ())), preferred_element_type=f32)


def block_step(k, m_ref, w_ref, g_ref, rhs_ref):
    t, o = divmod(k, 128)
    lane = lax.broadcasted_iota(jnp.int32, (1, 8, 128), 2)
    nth = lax.broadcasted_iota(jnp.int32, (BK, 8, 128), 0)
    R = [
        jnp.stack([jnp.broadcast_to(m_ref[k + i : k + i + 1, c * 128 : c * 128 + 128], (8, 128)) for i in range(BK)])
        for c in range(2)
    ]
    S = [jnp.broadcast_to(R[t][j:, :, o + j : o + j + 1], (BK - j, 8, 128)) for j in range(BK)]
    R[t] = jnp.where((lane >= o) & (lane < o + BK), jnp.where(lane - o == nth, 1.0, 0.0), R[t])
    inv, F, out = [], [], [[], []]
    for j in range(BK):
        inv.append(1.0 / S[j][0:1])
        for c in range(2):
            out[c].append(R[c][0:1])
        if j == BK - 1:
            break
        f = S[j][1:] * inv[j]
        for n in range(j + 1, BK):
            S[n] = S[n] - f[n - j - 1 :] * S[j][n - j : n - j + 1]
        R = [R[c][1:] - f * R[c][0:1] for c in range(2)]
        F.append(f)
    piv = jnp.concatenate([S[j][0:1] for j in range(BK)], 0)
    rs = lax.rsqrt(piv)
    U = [jnp.concatenate(out[c], 0) for c in range(2)]
    for c in range(2):
        v = U[c] * rs
        if c == t:
            v = jnp.where(lane < o + BK, v, 0.0)
        elif c > t:
            v = jnp.zeros_like(v)
        for i in range(BK):
            w_ref[k + i : k + i + 1, c * 128 : c * 128 + 128] = v[i, 0:1]
    if k + BK >= NB:
        return
    iv = jnp.concatenate(inv, 0)
    Z = [U[c] * iv for c in range(2)]
    for i in reversed(range(BK)):
        for c in range(2):
            g_ref[i : i + 1, c * 128 : c * 128 + 128] = Z[c][i, 0:1]
        if i:
            f = jnp.concatenate([F[n][i - n - 1 : i - n] for n in range(i)], 0)
            Z = [Z[c][:i] - f * Z[c][i : i + 1] for c in range(2)]
    gh, gm, gl = split3(g_ref[...])
    for q, (a, b) in enumerate(((gh, gh), (gm, gm), (gl, gh))):
        rhs_ref[q, o : o + BK, :] = a
        rhs_ref[q, 128 + o : 128 + o + BK, :] = b
    n0 = k + BK
    h, m, l = split3(m_ref[n0:NB, t * 128 : t * 128 + 128])
    hm = jnp.concatenate([h, m], 1)
    up = dot(hm, rhs_ref[0]) + dot(hm, rhs_ref[1])
    up = up + dot(jnp.concatenate([h, l], 1), rhs_ref[2])
    lanes = lax.broadcasted_iota(jnp.int32, (NB - n0, NB), 1)
    old = jnp.where((lanes >= k) & (lanes < k + BK), 0.0, m_ref[n0:NB, :])
    m_ref[n0:NB, :] = old - up
    zero = jnp.zeros((BK, NB), bf16)
    for q in range(3):
        rhs_ref[q, o : o + BK, :] = zero
        rhs_ref[q, 128 + o : 128 + o + BK, :] = zero


class Torus:
    def __init__(self):
        row, col = lax.axis_index("row"), lax.axis_index("col")
        self.x, self.y = row // 4, row % 4
        self.z, self.c = col // 2, col % 2

    def at(self, x=None, y=None, z=None, c=None):
        x = self.x if x is None else x
        y = self.y if y is None else y
        z = self.z if z is None else z
        c = self.c if c is None else c
        return {"row": x * 4 + y, "col": z * 2 + c}

    def step(self, dim, by):
        return self.at(**{dim: (getattr(self, dim) + by) % 4})

    def origin(self, y):
        same = jnp.where(y // 2 == self.c, 1, 0)
        return jnp.where(same == 1, y, 3 - y) % 2, 1 - same


NSEM = 37


class Share:
    def __init__(self, me, half, row_ref, col_ref, send, recv):
        self.me = me
        self.row, self.col = row_ref.at[half], col_ref.at[half]
        self.send, self.recv = send.at[half], recv.at[half]
        self.started = []

    def copy(self, ref, sem, to):
        return pltpu.make_async_remote_copy(
            src_ref=ref,
            dst_ref=ref,
            send_sem=self.send.at[sem],
            recv_sem=self.recv.at[sem],
            device_id=to,
            device_id_type=MESH,
        )

    def go(self, ref, sem, to):
        cp = self.copy(ref, sem, to)
        cp.start()
        self.started.append(cp)

    def wait(self, ref, sem):
        self.copy(ref, sem, self.me.step("x", 1)).wait_recv()

    def chunk(self, part, e=0, d=0):
        me = self.me
        back = (e, d) if part == 0 else (d, e)
        hx, hy = (me.x + 4 - back[0]) % 4, (me.y + 4 - back[1]) % 4
        yy, cc = me.origin(hy)
        return self.col.at[yy, hx, cc, part]

    def rowblock(self, d=0, e=0):
        me = self.me
        return self.row.at[2 * ((me.z + 4 - d) % 4) + (me.c + e) % 2]

    def second(self, part, e):
        for d in range(1, 4):
            self.go(self.chunk(part, e), 6 + 12 * part + 3 * e + d - 1, self.me.step("yx"[part], d))

    def begin(self):
        for part in range(2):
            for d in range(1, 4):
                self.go(self.chunk(part), 3 * part + d - 1, self.me.step("xy"[part], d))
        for part in range(2):
            self.second(part, 0)

    def others(self):
        return [(d, e) for d in range(4) for e in range(2) if d or e]

    def rows(self):
        me = self.me
        for i, (d, e) in enumerate(self.others()):
            self.go(self.rowblock(), 30 + i, me.at(z=(me.z + d) % 4, c=(me.c + e) % 2))

    def relay(self):
        for e in (1, 3, 2):
            for part in range(2):
                self.wait(self.chunk(part, e), 3 * part + e - 1)
                self.second(part, e)

    def finish(self):
        for i, (d, e) in enumerate(self.others()):
            self.wait(self.rowblock(d, e), 30 + i)
        for e in (0, 1, 3, 2):
            for part in range(2):
                for d in range(1, 4):
                    self.wait(self.chunk(part, e, d), 6 + 12 * part + 3 * e + d - 1)
        for cp in self.started:
            cp.wait_send()


def greet(me):
    barrier = pltpu.get_barrier_semaphore()

    def tell(to):
        pl.semaphore_signal(barrier, inc=1, device_id=to, device_id_type=MESH)

    same = jnp.where(me.y // 2 == me.c, 1, 0)
    me.own = (me.x == me.z) & (me.y // 2 == me.c) & (me.c == 0)
    me.other = jnp.logical_not(me.own)
    source = me.at(me.z, jnp.where(same == 1, me.y, 3 - me.y), me.x, 1 - same)
    pl.when(me.other)(lambda: tell(source))
    for d in range(4):
        for e in range(2):
            if d or e:
                tell(me.at(z=(me.z + d) % 4, c=(me.c + e) % 2))
    for dim in "xy":
        for d in range(1, 4):
            tell(me.step(dim, d))
    return barrier, 14 - jnp.where(me.own, 1, 0)


def panel_kernel(
    a_hbm, b_hbm, v_hbm, t_hbm, r_hbm, panel_ref, white_ref, wh_ref, row_ref, col_ref, t_ref, r_ref,
    m_ref, w_ref, g_ref, rhs_ref, bv_ref, held_ref, send, recv, first, local,
):
    loads = [
        pltpu.make_async_copy(a_hbm, m_ref, local.at[0]),
        pltpu.make_async_copy(b_hbm, bv_ref.at[0:RB], local.at[1]),
        pltpu.make_async_copy(v_hbm, bv_ref.at[RB:NB], local.at[2]),
    ]
    for cp in loads:
        cp.start()
    me = Torus()
    barrier, count = greet(me)
    rhs_ref[...] = jnp.zeros_like(rhs_ref)
    shares = [Share(me, h, row_ref, col_ref, send, recv) for h in range(2)]
    holder = me.at(me.z, jnp.where(me.c == 0, me.y, 3 - me.y), me.x, me.y // 2)
    raw = []
    for h in range(2):
        src = b_hbm.at[:, h * 128 : h * 128 + 128]
        raw.append(
            pltpu.make_async_remote_copy(
                src_ref=src,
                dst_ref=held_ref.at[h],
                send_sem=first.at[2 + h],
                recv_sem=first.at[h],
                device_id=holder,
                device_id_type=MESH,
            )
        )
    loads[0].wait()
    later = [pltpu.make_async_copy(t_hbm, t_ref, local.at[3]), pltpu.make_async_copy(r_hbm, r_ref, local.at[4])]
    for cp in later:
        cp.start()

    def solve(b, w):
        n = b.shape[1]
        bh, bm, _ = split3(b)
        wh, wm, _ = split3(w)
        return dot_nt(bh, wh) + (dot_nt(bh, wm) + dot_nt(bm, wh))

    def part_of(half):
        c0, n = half * 128, half * 128 + 128
        w = w_ref[c0:n, 0:n]
        raw[half].wait_recv()
        if half == 0:
            b = held_ref[0]
        else:
            b = jnp.concatenate([held_ref[0], held_ref[1]], 1)
        xb = solve(b, w).astype(bf16)
        for part in range(2):
            shares[half].chunk(part)[...] = xb[part * 96 : part * 96 + 96]
        if half == 0:
            loads[1].wait()
            loads[2].wait()
        x = solve(bv_ref[:, 0:n], w)
        xb = x.astype(bf16)
        for part in range(2):
            row_ref[half, 2 * me.z + me.c, part] = xb[part * 96 : part * 96 + 96]
        shares[half].begin()
        panel_ref[:, c0:n] = x[0:RB]
        white_ref[:, c0:n] = x[RB:NB]
        wh_ref[:, c0:n] = xb[RB:NB]
        shares[half].rows()

    for i in range(NB // BK):
        block_step(i * BK, m_ref, w_ref, g_ref, rhs_ref)
        if i == 0:
            pl.semaphore_wait(barrier, count)

            @pl.when(me.other)
            def _():
                for cp in raw:
                    cp.start()

            @pl.when(me.own)
            def _():
                for h in range(2):
                    pltpu.make_async_copy(b_hbm.at[:, h * 128 : h * 128 + 128], held_ref.at[h], first.at[h]).start()

        if i == SEND_AFTER:
            part_of(0)
        if i == RELAY_AFTER:
            shares[0].relay()
    part_of(1)
    shares[1].relay()
    for s in shares:
        s.finish()

    @pl.when(me.other)
    def _():
        for cp in raw:
            cp.wait_send()

    for cp in later:
        cp.wait()


def update_kernel(row_ref, col_ref, t_ref, wh_ref, v_ref, p_in, w_in, out_ref, vec_ref, p_ref, w_ref):
    i = pl.program_id(0)
    tm = out_ref.shape[0]
    rs = pl.ds(pl.multiple_of(i * tm, tm), tm)
    r = jnp.concatenate([row_ref[0, rs, :], row_ref[1, rs, :]], 1)
    c = jnp.concatenate([col_ref[0], col_ref[1]], 1)
    out_ref[...] = (t_ref[rs, :].astype(f32) - dot_nt(r, c)).astype(bf16)

    @pl.when(i == 0)
    def _():
        full = jnp.concatenate([row_ref[0], row_ref[1]], 1)
        vec_ref[...] = v_ref[...] - dot_nt(wh_ref[...], full)
        p_ref[...] = p_in[...]
        w_ref[...] = w_in[...]


VM = pl.BlockSpec(memory_space=pltpu.VMEM)
HB = pl.BlockSpec(memory_space=pltpu.MemorySpace.HBM)
SEND_AFTER, RELAY_AFTER = 9, 14


def per_device(diag_tile, panel_block, trailing, vec_head, vec_rest):
    nv = vec_head.shape[0]
    mr, mc = trailing.shape
    inputs = [
        pltpu.with_memory_space_constraint(a, pltpu.MemorySpace.HBM)
        for a in (diag_tile, panel_block, vec_head, trailing, vec_rest)
    ]
    panel, white, wh, rowp, colp, tiles, rest = pl.pallas_call(
        panel_kernel,
        out_shape=(
            jax.ShapeDtypeStruct((RB, NB), f32),
            jax.ShapeDtypeStruct((nv, NB), f32),
            jax.ShapeDtypeStruct((nv, NB), bf16),
            jax.ShapeDtypeStruct((2, 8, 2, 96, 128), bf16),
            jax.ShapeDtypeStruct((2, 2, 4, 2, 2, 96, 128), bf16),
            jax.ShapeDtypeStruct((mr, mc), bf16),
            jax.ShapeDtypeStruct((nv, mr), f32),
        ),
        in_specs=[HB] * 5,
        out_specs=(VM,) * 7,
        scratch_shapes=[
            pltpu.VMEM((NB, NB), f32),
            pltpu.VMEM((NB, NB), f32),
            pltpu.VMEM((BK, NB), f32),
            pltpu.VMEM((3, NB, NB), bf16),
            pltpu.VMEM((NB, NB), f32),
            pltpu.VMEM((2, RB, 128), f32),
            pltpu.SemaphoreType.DMA((2, NSEM)),
            pltpu.SemaphoreType.DMA((2, NSEM)),
            pltpu.SemaphoreType.DMA((4,)),
            pltpu.SemaphoreType.DMA((5,)),
        ],
        compiler_params=pltpu.CompilerParams(
            collective_id=0, has_side_effects=True, vmem_limit_bytes=12 * MIB
        ),
        cost_estimate=pl.CostEstimate(flops=20 * 10**9, bytes_accessed=0, transcendentals=0),
        name="panel",
    )(*inputs)
    rowp = rowp.reshape(2, mr, 128)
    colp = colp.reshape(2, mc, 128)
    tm = 384
    whole = lambda shape: pl.BlockSpec(shape, lambda i: (0, 0))
    out, vec, panel, white = pl.pallas_call(
        update_kernel,
        grid=(mr // tm,),
        out_shape=(
            jax.ShapeDtypeStruct((mr, mc), bf16),
            jax.ShapeDtypeStruct((nv, mr), f32),
            jax.ShapeDtypeStruct((RB, NB), f32),
            jax.ShapeDtypeStruct((nv, NB), f32),
        ),
        in_specs=[VM] * 7,
        out_specs=(
            pl.BlockSpec((tm, mc), lambda i: (i, 0)),
            whole((nv, mr)),
            whole((RB, NB)),
            whole((nv, NB)),
        ),
        compiler_params=pltpu.CompilerParams(vmem_limit_bytes=40 * MIB),
        name="update",
    )(rowp, colp, tiles, wh, rest, panel, white)
    return (panel, out, white, vec)


def solution(mesh):
    in_specs = (P(), P(("row", "col"), None), P("row", "col"), P("col", None), P("col", "row"))
    out_specs = (P(("row", "col"), None), P("row", "col"), P("col", None), P("col", "row"))
    return jax.shard_map(per_device, mesh=mesh, in_specs=in_specs, out_specs=out_specs, check_vma=False)
```

```python
import jax
import jax.numpy as jnp
from jax import lax
from jax.experimental import pallas as pl
from jax.experimental.pallas import tpu as pltpu
from jax.sharding import PartitionSpec as P

f32, bf16 = jnp.float32, jnp.bfloat16
MESH = pl.DeviceIdType.MESH
BK = 16
NB = 256
RB = 192
MIB = 1 << 20


def split3(x):
    h = x.astype(bf16)
    r = x - h.astype(f32)
    m = r.astype(bf16)
    return h, m, (r - m.astype(f32)).astype(bf16)


def dot(a, b):
    return lax.dot_general(a, b, (((1,), (0,)), ((), ())), preferred_element_type=f32)


def dot_nt(a, b):
    return lax.dot_general(a, b, (((1,), (1,)), ((), ())), preferred_element_type=f32)


def block_step(k, m_ref, w_ref, g_ref, rhs_ref):
    t, o = divmod(k, 128)
    lane = lax.broadcasted_iota(jnp.int32, (1, 8, 128), 2)
    tile = lax.broadcasted_iota(jnp.int32, (1, 8, 128), 1) // 4
    nth = lax.broadcasted_iota(jnp.int32, (BK, 8, 128), 0)
    T = [
        jnp.stack([jnp.broadcast_to(m_ref[k + i : k + i + 1, c * 128 : c * 128 + 128], (8, 128)) for i in range(BK)])
        for c in range(2)
    ]
    S = [jnp.broadcast_to(T[t][j:, :, o + j : o + j + 1], (BK - j, 8, 128)) for j in range(BK)]
    R = jnp.where(tile == 0, T[0], T[1])
    at = lane + 128 * tile - k
    R = jnp.where((at >= 0) & (at < BK), jnp.where(at == nth, 1.0, 0.0), R)
    inv, F, out = [], [], []
    for j in range(BK):
        inv.append(1.0 / S[j][0:1])
        out.append(R[0:1])
        if j == BK - 1:
            break
        f = S[j][1:] * inv[j]
        for n in range(j + 1, BK):
            S[n] = S[n] - f[n - j - 1 :] * S[j][n - j : n - j + 1]
        R = R[1:] - f * R[0:1]
        F.append(f)
    rs = lax.rsqrt(jnp.concatenate([S[j][0:1] for j in range(BK)], 0))
    U = jnp.concatenate(out, 0)
    v = jnp.where(at < BK, U * rs, 0.0)
    for i in range(BK):
        for c in range(2):
            w_ref[k + i : k + i + 1, c * 128 : c * 128 + 128] = v[i, 4 * c : 4 * c + 1]
    if k + BK >= NB:
        return
    Z = U * jnp.concatenate(inv, 0)
    for i in reversed(range(BK)):
        for c in range(2):
            g_ref[i : i + 1, c * 128 : c * 128 + 128] = Z[i, 4 * c : 4 * c + 1]
        if i:
            f = jnp.concatenate([F[n][i - n - 1 : i - n] for n in range(i)], 0)
            Z = Z[:i] - f * Z[i : i + 1]
    gh, gm, gl = split3(g_ref[...])
    for q, a in enumerate((gh, gh, gm, gm, gl, gh)):
        rhs_ref[q * 128 + o : q * 128 + o + BK, :] = a
    n0 = k + BK
    h, m, l = split3(m_ref[n0:NB, t * 128 : t * 128 + 128])
    up = dot(jnp.concatenate([h, m, h, m, h, l], 1), rhs_ref[...])
    lanes = lax.broadcasted_iota(jnp.int32, (NB - n0, NB), 1)
    old = jnp.where((lanes >= k) & (lanes < k + BK), 0.0, m_ref[n0:NB, :])
    m_ref[n0:NB, :] = old - up
    zero = jnp.zeros((BK, NB), bf16)
    for q in range(6):
        rhs_ref[q * 128 + o : q * 128 + o + BK, :] = zero


class Torus:
    def __init__(self):
        row, col = lax.axis_index("row"), lax.axis_index("col")
        self.x, self.y = row // 4, row % 4
        self.z, self.c = col // 2, col % 2

    def at(self, x=None, y=None, z=None, c=None):
        x = self.x if x is None else x
        y = self.y if y is None else y
        z = self.z if z is None else z
        c = self.c if c is None else c
        return {"row": x * 4 + y, "col": z * 2 + c}

    def step(self, dim, by):
        return self.at(**{dim: (getattr(self, dim) + by) % 4})

    def origin(self, y):
        same = jnp.where(y // 2 == self.c, 1, 0)
        return jnp.where(same == 1, y, 3 - y) % 2, 1 - same


NSEM = 45


class Share:
    def __init__(self, me, half, row_ref, col_ref, send, recv):
        self.me, self.ring = me, half == 0
        self.row, self.col = row_ref.at[half], col_ref.at[half]
        self.send, self.recv = send.at[half], recv.at[half]
        self.started = []

    def copy(self, ref, sem, to):
        return pltpu.make_async_remote_copy(
            src_ref=ref,
            dst_ref=ref,
            send_sem=self.send.at[sem],
            recv_sem=self.recv.at[sem],
            device_id=to,
            device_id_type=MESH,
        )

    def go(self, ref, sem, to):
        cp = self.copy(ref, sem, to)
        cp.start()
        self.started.append(cp)

    def wait(self, ref, sem):
        self.copy(ref, sem, self.me.step("x", 1)).wait_recv()

    def chunk(self, part, e=0, d=0):
        me = self.me
        back = (e, d) if part == 0 else (d, e)
        hx, hy = (me.x + 4 - back[0]) % 4, (me.y + 4 - back[1]) % 4
        yy, cc = me.origin(hy)
        return self.col.at[yy, hx, cc, part]

    def rowblock(self, d=0, e=0):
        me = self.me
        return self.row.at[2 * ((me.z + 4 - d) % 4) + (me.c + e) % 2]

    def second(self, part, e):
        for d in (1, 3) if self.ring else (2, 1, 3):
            self.go(self.chunk(part, e), 6 + 12 * part + 3 * e + d - 1, self.me.step("yx"[part], d))

    def begin(self):
        for part in range(2):
            for d in (2, 1, 3):
                self.go(self.chunk(part), 3 * part + d - 1, self.me.step("xy"[part], d))
        for part in range(2):
            self.second(part, 0)

    def others(self):
        return [(d, e) for d in range(4) for e in range(2) if d or e]

    def rows(self):
        me = self.me
        for i, (d, e) in enumerate(self.others()):
            self.go(self.rowblock(), 30 + i, me.at(z=(me.z + d) % 4, c=(me.c + e) % 2))

    def relay(self):
        for e in (1, 3, 2):
            for part in range(2):
                self.wait(self.chunk(part, e), 3 * part + e - 1)
                self.second(part, e)

    def far(self, part, e, which):
        return self.chunk(part, e, 2).at[which * 48 : which * 48 + 48], (6 + 12 * part + 3 * e + 1, 37 + 4 * part + e)[which]

    def forward(self):
        for e in (0, 1, 3, 2):
            for part in range(2):
                for which, d in enumerate((1, 3)):
                    whole = self.chunk(part, e, d)
                    self.wait(whole, 6 + 12 * part + 3 * e + d - 1)
                    self.go(whole.at[which * 48 : which * 48 + 48], self.far(part, e, which)[1], self.me.step("yx"[part], d))

    def finish(self):
        for i, (d, e) in enumerate(self.others()):
            self.wait(self.rowblock(d, e), 30 + i)
        for e in (0, 1, 3, 2):
            for part in range(2):
                if self.ring:
                    for which in range(2):
                        self.wait(*self.far(part, e, which))
                    continue
                for d in range(1, 4):
                    self.wait(self.chunk(part, e, d), 6 + 12 * part + 3 * e + d - 1)
        for cp in self.started:
            cp.wait_send()


def greet(me):
    barrier = pltpu.get_barrier_semaphore()

    def tell(to):
        pl.semaphore_signal(barrier, inc=1, device_id=to, device_id_type=MESH)

    same = jnp.where(me.y // 2 == me.c, 1, 0)
    me.own = (me.x == me.z) & (me.y // 2 == me.c) & (me.c == 0)
    me.other = jnp.logical_not(me.own)
    source = me.at(me.z, jnp.where(same == 1, me.y, 3 - me.y), me.x, 1 - same)
    pl.when(me.other)(lambda: tell(source))
    for d in range(4):
        for e in range(2):
            if d or e:
                tell(me.at(z=(me.z + d) % 4, c=(me.c + e) % 2))
    for dim in "xy":
        for d in range(1, 4):
            tell(me.step(dim, d))
    return barrier, 14 - jnp.where(me.own, 1, 0)


def panel_kernel(
    a_hbm, b_hbm, v_hbm, t_hbm, r_hbm, panel_ref, white_ref, wh_ref, row_ref, col_ref, t_ref, r_ref,
    m_ref, w_ref, g_ref, rhs_ref, bv_ref, held_ref, send, recv, first, local,
):
    me = Torus()
    barrier, count = greet(me)
    holder = me.at(me.z, jnp.where(me.c == 0, me.y, 3 - me.y), me.x, me.y // 2)
    halves = [b_hbm.at[:, h * 128 : h * 128 + 128] for h in range(2)]
    spans = [w_ref.at[0:128, 0:128], w_ref.at[128:NB]]

    def flow(lead):
        loads = [
            pltpu.make_async_copy(b_hbm, bv_ref.at[0:RB], local.at[1]),
            pltpu.make_async_copy(v_hbm, bv_ref.at[RB:NB], local.at[2]),
        ]
        later = [pltpu.make_async_copy(t_hbm, t_ref, local.at[3]), pltpu.make_async_copy(r_hbm, r_ref, local.at[4])]
        shares = [Share(me, h, row_ref, col_ref, send, recv) for h in range(2)]
        raw = [
            pltpu.make_async_remote_copy(
                src_ref=halves[h],
                dst_ref=held_ref.at[h],
                send_sem=first.at[2 + h],
                recv_sem=first.at[h],
                device_id=holder,
                device_id_type=MESH,
            )
            for h in range(2)
        ]
        gift = [
            pltpu.make_async_remote_copy(
                src_ref=spans[h],
                dst_ref=spans[h],
                send_sem=first.at[6 + h],
                recv_sem=first.at[4 + h],
                device_id=me.at(c=1 - me.c),
                device_id_type=MESH,
            )
            for h in range(2)
        ]

        def enter():
            pl.semaphore_wait(barrier, count)

            @pl.when(me.other)
            def _():
                for cp in raw:
                    cp.start()

            @pl.when(me.own)
            def _():
                for h in range(2):
                    pltpu.make_async_copy(halves[h], held_ref.at[h], first.at[h]).start()

        def solve(b, w):
            bh, bm, _ = split3(b)
            wh, wm, _ = split3(w)
            return dot_nt(bh, wh) + (dot_nt(bh, wm) + dot_nt(bm, wh))

        def part_of(half):
            c0, n = half * 128, half * 128 + 128
            raw[half].wait_recv()
            if not lead:
                gift[half].wait_recv()
            w = w_ref[c0:n, 0:n]
            if half == 0:
                b = held_ref[0]
            else:
                b = jnp.concatenate([held_ref[0], held_ref[1]], 1)
            xb = solve(b, w).astype(bf16)
            for part in range(2):
                shares[half].chunk(part)[...] = xb[part * 96 : part * 96 + 96]
            if lead and half == 1:
                gift[1].start()
            if half == 0:
                for cp in loads:
                    cp.wait()
            x = solve(bv_ref[:, 0:n], w)
            xb = x.astype(bf16)
            for part in range(2):
                row_ref[half, 2 * me.z + me.c, part] = xb[part * 96 : part * 96 + 96]
            shares[half].begin()
            panel_ref[:, c0:n] = x[0:RB]
            white_ref[:, c0:n] = x[RB:NB]
            wh_ref[:, c0:n] = xb[RB:NB]
            shares[half].rows()

        if lead:
            diag = pltpu.make_async_copy(a_hbm, m_ref, local.at[0])
            diag.start()
            for cp in loads:
                cp.start()
            rhs_ref[...] = jnp.zeros_like(rhs_ref)
            diag.wait()
            for cp in later:
                cp.start()
            for i in range(NB // BK):
                block_step(i * BK, m_ref, w_ref, g_ref, rhs_ref)
                if i == 0:
                    enter()
                if i == 8:
                    gift[0].start()
                if i == SEND_AFTER:
                    part_of(0)
                if i == RELAY_AFTER:
                    shares[0].relay()
        else:
            enter()
            for cp in loads + later:
                cp.start()
            part_of(0)
            shares[0].relay()
        part_of(1)
        if lead and RELAY_AFTER > 15:
            shares[0].relay()
        shares[0].forward()
        shares[1].relay()
        for s in shares:
            s.finish()
        if lead:
            for cp in gift:
                cp.wait_send()

        @pl.when(me.other)
        def _():
            for cp in raw:
                cp.wait_send()

        for cp in later:
            cp.wait()

    pl.when(me.c == 0)(lambda: flow(True))
    pl.when(me.c == 1)(lambda: flow(False))


def update_kernel(row_ref, col_ref, t_ref, wh_ref, v_ref, p_in, w_in, out_ref, vec_ref, p_ref, w_ref):
    i = pl.program_id(0)
    tm = out_ref.shape[0]
    rs = pl.ds(pl.multiple_of(i * tm, tm), tm)
    r = jnp.concatenate([row_ref[0, rs, :], row_ref[1, rs, :]], 1)
    c = jnp.concatenate([col_ref[0], col_ref[1]], 1)
    out_ref[...] = (t_ref[rs, :].astype(f32) - dot_nt(r, c)).astype(bf16)

    @pl.when(i == 0)
    def _():
        full = jnp.concatenate([row_ref[0], row_ref[1]], 1)
        vec_ref[...] = v_ref[...] - dot_nt(wh_ref[...], full)
        p_ref[...] = p_in[...]
        w_ref[...] = w_in[...]


VM = pl.BlockSpec(memory_space=pltpu.VMEM)
HB = pl.BlockSpec(memory_space=pltpu.MemorySpace.HBM)
SEND_AFTER, RELAY_AFTER = 14, 16


def per_device(diag_tile, panel_block, trailing, vec_head, vec_rest):
    nv = vec_head.shape[0]
    mr, mc = trailing.shape
    inputs = [
        pltpu.with_memory_space_constraint(a, pltpu.MemorySpace.HBM)
        for a in (diag_tile, panel_block, vec_head, trailing, vec_rest)
    ]
    panel, white, wh, rowp, colp, tiles, rest = pl.pallas_call(
        panel_kernel,
        out_shape=(
            jax.ShapeDtypeStruct((RB, NB), f32),
            jax.ShapeDtypeStruct((nv, NB), f32),
            jax.ShapeDtypeStruct((nv, NB), bf16),
            jax.ShapeDtypeStruct((2, 8, 2, 96, 128), bf16),
            jax.ShapeDtypeStruct((2, 2, 4, 2, 2, 96, 128), bf16),
            jax.ShapeDtypeStruct((mr, mc), bf16),
            jax.ShapeDtypeStruct((nv, mr), f32),
        ),
        in_specs=[HB] * 5,
        out_specs=(VM,) * 7,
        scratch_shapes=[
            pltpu.VMEM((NB, NB), f32),
            pltpu.VMEM((NB, NB), f32),
            pltpu.VMEM((BK, NB), f32),
            pltpu.VMEM((3 * NB, NB), bf16),
            pltpu.VMEM((NB, NB), f32),
            pltpu.VMEM((2, RB, 128), f32),
            pltpu.SemaphoreType.DMA((2, NSEM)),
            pltpu.SemaphoreType.DMA((2, NSEM)),
            pltpu.SemaphoreType.DMA((8,)),
            pltpu.SemaphoreType.DMA((5,)),
        ],
        compiler_params=pltpu.CompilerParams(
            collective_id=0, has_side_effects=True, vmem_limit_bytes=12 * MIB
        ),
        cost_estimate=pl.CostEstimate(flops=20 * 10**9, bytes_accessed=0, transcendentals=0),
        name="panel",
    )(*inputs)
    rowp = rowp.reshape(2, mr, 128)
    colp = colp.reshape(2, mc, 128)
    tm = 384
    whole = lambda shape: pl.BlockSpec(shape, lambda i: (0, 0))
    out, vec, panel, white = pl.pallas_call(
        update_kernel,
        grid=(mr // tm,),
        out_shape=(
            jax.ShapeDtypeStruct((mr, mc), bf16),
            jax.ShapeDtypeStruct((nv, mr), f32),
            jax.ShapeDtypeStruct((RB, NB), f32),
            jax.ShapeDtypeStruct((nv, NB), f32),
        ),
        in_specs=[VM] * 7,
        out_specs=(
            pl.BlockSpec((tm, mc), lambda i: (i, 0)),
            whole((nv, mr)),
            whole((RB, NB)),
            whole((nv, NB)),
        ),
        compiler_params=pltpu.CompilerParams(vmem_limit_bytes=40 * MIB),
        name="update",
    )(rowp, colp, tiles, wh, rest, panel, white)
    return (panel, out, white, vec)


def solution(mesh):
    in_specs = (P(), P(("row", "col"), None), P("row", "col"), P("col", None), P("col", "row"))
    out_specs = (P(("row", "col"), None), P("row", "col"), P("col", None), P("col", "row"))
    return jax.shard_map(per_device, mesh=mesh, in_specs=in_specs, out_specs=out_specs, check_vma=False)
```

```python
import jax
import jax.numpy as jnp
from jax import lax
from jax.experimental import pallas as pl
from jax.experimental.pallas import tpu as pltpu
from jax.sharding import PartitionSpec as P

f32, bf16 = jnp.float32, jnp.bfloat16
MESH = pl.DeviceIdType.MESH
BK = 16
NB = 256
RB = 192
MIB = 1 << 20


def split3(x):
    h = x.astype(bf16)
    r = x - h.astype(f32)
    m = r.astype(bf16)
    return h, m, (r - m.astype(f32)).astype(bf16)


def dot(a, b):
    return lax.dot_general(a, b, (((1,), (0,)), ((), ())), preferred_element_type=f32)


def dot_nt(a, b):
    return lax.dot_general(a, b, (((1,), (1,)), ((), ())), preferred_element_type=f32)


def block_step(k, m_ref, w_ref, g_ref, rhs_ref):
    t, o = divmod(k, 128)
    lane = lax.broadcasted_iota(jnp.int32, (1, 8, 128), 2)
    tile = lax.broadcasted_iota(jnp.int32, (1, 8, 128), 1) // 4
    nth = lax.broadcasted_iota(jnp.int32, (BK, 8, 128), 0)
    T = [
        jnp.stack([jnp.broadcast_to(m_ref[k + i : k + i + 1, c * 128 : c * 128 + 128], (8, 128)) for i in range(BK)])
        for c in range(2)
    ]
    S = [jnp.broadcast_to(T[t][j:, :, o + j : o + j + 1], (BK - j, 8, 128)) for j in range(BK)]
    R = jnp.where(tile == 0, T[0], T[1])
    at = lane + 128 * tile - k
    R = jnp.where((at >= 0) & (at < BK), jnp.where(at == nth, 1.0, 0.0), R)
    inv, F, out = [], [], []
    for j in range(BK):
        inv.append(1.0 / S[j][0:1])
        out.append(R[0:1])
        if j == BK - 1:
            break
        f = S[j][1:] * inv[j]
        for n in range(j + 1, BK):
            S[n] = S[n] - f[n - j - 1 :] * S[j][n - j : n - j + 1]
        R = R[1:] - f * R[0:1]
        F.append(f)
    rs = lax.rsqrt(jnp.concatenate([S[j][0:1] for j in range(BK)], 0))
    U = jnp.concatenate(out, 0)
    v = jnp.where(at < BK, U * rs, 0.0)
    for i in range(BK):
        for c in range(2):
            w_ref[k + i : k + i + 1, c * 128 : c * 128 + 128] = v[i, 4 * c : 4 * c + 1]
    if k + BK >= NB:
        return
    Z = U * jnp.concatenate(inv, 0)
    for i in reversed(range(BK)):
        for c in range(2):
            g_ref[i : i + 1, c * 128 : c * 128 + 128] = Z[i, 4 * c : 4 * c + 1]
        if i:
            f = jnp.concatenate([F[n][i - n - 1 : i - n] for n in range(i)], 0)
            Z = Z[:i] - f * Z[i : i + 1]
    gh, gm, gl = split3(g_ref[...])
    for q, a in enumerate((gh, gh, gm, gm, gl, gh)):
        rhs_ref[q * 128 + o : q * 128 + o + BK, :] = a
    n0 = k + BK
    h, m, l = split3(m_ref[n0:NB, t * 128 : t * 128 + 128])
    up = dot(jnp.concatenate([h, m, h, m, h, l], 1), rhs_ref[...])
    lanes = lax.broadcasted_iota(jnp.int32, (NB - n0, NB), 1)
    old = jnp.where((lanes >= k) & (lanes < k + BK), 0.0, m_ref[n0:NB, :])
    m_ref[n0:NB, :] = old - up
    zero = jnp.zeros((BK, NB), bf16)
    for q in range(6):
        rhs_ref[q * 128 + o : q * 128 + o + BK, :] = zero


class Torus:
    def __init__(self):
        row, col = lax.axis_index("row"), lax.axis_index("col")
        self.x, self.y = row // 4, row % 4
        self.z, self.c = col // 2, col % 2

    def at(self, x=None, y=None, z=None, c=None):
        x = self.x if x is None else x
        y = self.y if y is None else y
        z = self.z if z is None else z
        c = self.c if c is None else c
        return {"row": x * 4 + y, "col": z * 2 + c}

    def step(self, dim, by):
        return self.at(**{dim: (getattr(self, dim) + by) % 4})

    def origin(self, y):
        same = jnp.where(y // 2 == self.c, 1, 0)
        return jnp.where(same == 1, y, 3 - y) % 2, 1 - same


NSEM = 45


class Share:
    def __init__(self, me, half, row_ref, col_ref, send, recv):
        self.me, self.ring, self.diag = me, half == 0, DIAG[half]
        self.row, self.col = row_ref.at[half], col_ref.at[half]
        self.send, self.recv = send.at[half], recv.at[half]
        self.started = []

    def copy(self, ref, sem, to):
        return pltpu.make_async_remote_copy(
            src_ref=ref,
            dst_ref=ref,
            send_sem=self.send.at[sem],
            recv_sem=self.recv.at[sem],
            device_id=to,
            device_id_type=MESH,
        )

    def go(self, ref, sem, to):
        cp = self.copy(ref, sem, to)
        cp.start()
        self.started.append(cp)

    def wait(self, ref, sem):
        self.copy(ref, sem, self.me.step("x", 1)).wait_recv()

    def chunk(self, part, e=0, d=0):
        me = self.me
        back = (e, d) if part == 0 else (d, e)
        hx, hy = (me.x + 4 - back[0]) % 4, (me.y + 4 - back[1]) % 4
        yy, cc = me.origin(hy)
        return self.col.at[yy, hx, cc, part]

    def rowblock(self, d=0, e=0):
        me = self.me
        return self.row.at[2 * ((me.z + 4 - d) % 4) + (me.c + e) % 2]

    def across(self, part):
        dims = "xy" if part == 0 else "yx"
        for e in (1, 3):
            for d in (1, 3):
                to = {dims[0]: (getattr(self.me, dims[0]) + e) % 4, dims[1]: (getattr(self.me, dims[1]) + d) % 4}
                self.go(self.chunk(part), 6 + 12 * part + 3 * e + d - 1, self.me.at(**to))

    def second(self, part, e):
        if self.diag and e in (1, 3):
            if not self.ring:
                self.go(self.chunk(part, e), 6 + 12 * part + 3 * e + 1, self.me.step("yx"[part], 2))
            return
        for d in (1, 3) if self.ring else (2, 1, 3):
            self.go(self.chunk(part, e), 6 + 12 * part + 3 * e + d - 1, self.me.step("yx"[part], d))

    def begin(self):
        for part in range(2):
            for d in (2, 1, 3):
                self.go(self.chunk(part), 3 * part + d - 1, self.me.step("xy"[part], d))
        for part in range(2):
            self.second(part, 0)
        if self.diag:
            for part in range(2):
                self.across(part)

    def others(self):
        return [(d, e) for d in range(4) for e in range(2) if d or e]

    def rows(self):
        me = self.me
        for i, (d, e) in enumerate(self.others()):
            self.go(self.rowblock(), 30 + i, me.at(z=(me.z + d) % 4, c=(me.c + e) % 2))

    def relay(self):
        for e in (1, 3, 2):
            for part in range(2):
                self.wait(self.chunk(part, e), 3 * part + e - 1)
                self.second(part, e)

    def far(self, part, e, which):
        return self.chunk(part, e, 2).at[which * 48 : which * 48 + 48], (6 + 12 * part + 3 * e + 1, 37 + 4 * part + e)[which]

    def forward(self):
        for e in (0, 1, 3, 2):
            for part in range(2):
                for which, d in enumerate((1, 3)):
                    whole = self.chunk(part, e, d)
                    self.wait(whole, 6 + 12 * part + 3 * e + d - 1)
                    self.go(whole.at[which * 48 : which * 48 + 48], self.far(part, e, which)[1], self.me.step("yx"[part], d))

    def finish(self):
        for i, (d, e) in enumerate(self.others()):
            self.wait(self.rowblock(d, e), 30 + i)
        for e in (0, 1, 3, 2):
            for part in range(2):
                if self.ring:
                    for which in range(2):
                        self.wait(*self.far(part, e, which))
                    continue
                for d in range(1, 4):
                    self.wait(self.chunk(part, e, d), 6 + 12 * part + 3 * e + d - 1)
        for cp in self.started:
            cp.wait_send()


def greet(me):
    barrier = pltpu.get_barrier_semaphore()

    def tell(to):
        pl.semaphore_signal(barrier, inc=1, device_id=to, device_id_type=MESH)

    same = jnp.where(me.y // 2 == me.c, 1, 0)
    me.own = (me.x == me.z) & (me.y // 2 == me.c) & (me.c == 0)
    me.other = jnp.logical_not(me.own)
    source = me.at(me.z, jnp.where(same == 1, me.y, 3 - me.y), me.x, 1 - same)
    pl.when(me.other)(lambda: tell(source))
    for d in range(4):
        for e in range(2):
            if d or e:
                tell(me.at(z=(me.z + d) % 4, c=(me.c + e) % 2))
    for dim in "xy":
        for d in range(1, 4):
            tell(me.step(dim, d))
    for e in (1, 3):
        for d in (1, 3):
            tell(me.at(x=(me.x + e) % 4, y=(me.y + d) % 4))
    return barrier, 18 - jnp.where(me.own, 1, 0)


def panel_kernel(
    a_hbm, b_hbm, v_hbm, t_hbm, r_hbm, panel_ref, white_ref, wh_ref, row_ref, col_ref, t_ref, r_ref,
    m_ref, w_ref, g_ref, rhs_ref, bv_ref, held_ref, send, recv, first, local,
):
    me = Torus()
    barrier, count = greet(me)
    holder = me.at(me.z, jnp.where(me.c == 0, me.y, 3 - me.y), me.x, me.y // 2)
    halves = [b_hbm.at[:, h * 128 : h * 128 + 128] for h in range(2)]
    spans = [w_ref.at[0:128, 0:128], w_ref.at[128:NB]]

    def flow(lead):
        loads = [
            pltpu.make_async_copy(b_hbm, bv_ref.at[0:RB], local.at[1]),
            pltpu.make_async_copy(v_hbm, bv_ref.at[RB:NB], local.at[2]),
        ]
        later = [pltpu.make_async_copy(t_hbm, t_ref, local.at[3]), pltpu.make_async_copy(r_hbm, r_ref, local.at[4])]
        shares = [Share(me, h, row_ref, col_ref, send, recv) for h in range(2)]
        raw = [
            pltpu.make_async_remote_copy(
                src_ref=halves[h],
                dst_ref=held_ref.at[h],
                send_sem=first.at[2 + h],
                recv_sem=first.at[h],
                device_id=holder,
                device_id_type=MESH,
            )
            for h in range(2)
        ]
        gift = [
            pltpu.make_async_remote_copy(
                src_ref=spans[h],
                dst_ref=spans[h],
                send_sem=first.at[6 + h],
                recv_sem=first.at[4 + h],
                device_id=me.at(c=1 - me.c),
                device_id_type=MESH,
            )
            for h in range(2)
        ]

        def enter():
            pl.semaphore_wait(barrier, count)

            @pl.when(me.other)
            def _():
                for cp in raw:
                    cp.start()

            @pl.when(me.own)
            def _():
                for h in range(2):
                    pltpu.make_async_copy(halves[h], held_ref.at[h], first.at[h]).start()

        def solve(b, w):
            bh, bm, _ = split3(b)
            wh, wm, _ = split3(w)
            return dot_nt(bh, wh) + (dot_nt(bh, wm) + dot_nt(bm, wh))

        def part_of(half):
            c0, n = half * 128, half * 128 + 128
            raw[half].wait_recv()
            if not lead:
                gift[half].wait_recv()
            w = w_ref[c0:n, 0:n]
            if half == 0:
                b = held_ref[0]
            else:
                b = jnp.concatenate([held_ref[0], held_ref[1]], 1)
            xb = solve(b, w).astype(bf16)
            for part in range(2):
                shares[half].chunk(part)[...] = xb[part * 96 : part * 96 + 96]
            if lead and half == 1:
                gift[1].start()
            if half == 0:
                for cp in loads:
                    cp.wait()
            x = solve(bv_ref[:, 0:n], w)
            xb = x.astype(bf16)
            for part in range(2):
                row_ref[half, 2 * me.z + me.c, part] = xb[part * 96 : part * 96 + 96]
            shares[half].begin()
            panel_ref[:, c0:n] = x[0:RB]
            white_ref[:, c0:n] = x[RB:NB]
            wh_ref[:, c0:n] = xb[RB:NB]
            shares[half].rows()

        if lead:
            diag = pltpu.make_async_copy(a_hbm, m_ref, local.at[0])
            diag.start()
            for cp in loads:
                cp.start()
            rhs_ref[...] = jnp.zeros_like(rhs_ref)
            diag.wait()
            for cp in later:
                cp.start()
            for i in range(NB // BK):
                block_step(i * BK, m_ref, w_ref, g_ref, rhs_ref)
                if i == 0:
                    enter()
                if i == 8:
                    gift[0].start()
                if i == SEND_AFTER:
                    part_of(0)
                if i == RELAY_AFTER:
                    shares[0].relay()
        else:
            enter()
            for cp in loads + later:
                cp.start()
            part_of(0)
            shares[0].relay()
        part_of(1)
        if lead and RELAY_AFTER > 15:
            shares[0].relay()
        shares[0].forward()
        shares[1].relay()
        for s in shares:
            s.finish()
        if lead:
            for cp in gift:
                cp.wait_send()

        @pl.when(me.other)
        def _():
            for cp in raw:
                cp.wait_send()

        for cp in later:
            cp.wait()

    pl.when(me.c == 0)(lambda: flow(True))
    pl.when(me.c == 1)(lambda: flow(False))


def update_kernel(row_ref, col_ref, t_ref, wh_ref, v_ref, p_in, w_in, out_ref, vec_ref, p_ref, w_ref):
    i = pl.program_id(0)
    tm = out_ref.shape[0]
    rs = pl.ds(pl.multiple_of(i * tm, tm), tm)
    r = jnp.concatenate([row_ref[0, rs, :], row_ref[1, rs, :]], 1)
    c = jnp.concatenate([col_ref[0], col_ref[1]], 1)
    out_ref[...] = (t_ref[rs, :].astype(f32) - dot_nt(r, c)).astype(bf16)

    @pl.when(i == 0)
    def _():
        full = jnp.concatenate([row_ref[0], row_ref[1]], 1)
        vec_ref[...] = v_ref[...] - dot_nt(wh_ref[...], full)
        p_ref[...] = p_in[...]
        w_ref[...] = w_in[...]


VM = pl.BlockSpec(memory_space=pltpu.VMEM)
HB = pl.BlockSpec(memory_space=pltpu.MemorySpace.HBM)
SEND_AFTER, RELAY_AFTER = 13, 16
DIAG = (True, False)


def per_device(diag_tile, panel_block, trailing, vec_head, vec_rest):
    nv = vec_head.shape[0]
    mr, mc = trailing.shape
    inputs = [
        pltpu.with_memory_space_constraint(a, pltpu.MemorySpace.HBM)
        for a in (diag_tile, panel_block, vec_head, trailing, vec_rest)
    ]
    panel, white, wh, rowp, colp, tiles, rest = pl.pallas_call(
        panel_kernel,
        out_shape=(
            jax.ShapeDtypeStruct((RB, NB), f32),
            jax.ShapeDtypeStruct((nv, NB), f32),
            jax.ShapeDtypeStruct((nv, NB), bf16),
            jax.ShapeDtypeStruct((2, 8, 2, 96, 128), bf16),
            jax.ShapeDtypeStruct((2, 2, 4, 2, 2, 96, 128), bf16),
            jax.ShapeDtypeStruct((mr, mc), bf16),
            jax.ShapeDtypeStruct((nv, mr), f32),
        ),
        in_specs=[HB] * 5,
        out_specs=(VM,) * 7,
        scratch_shapes=[
            pltpu.VMEM((NB, NB), f32),
            pltpu.VMEM((NB, NB), f32),
            pltpu.VMEM((BK, NB), f32),
            pltpu.VMEM((3 * NB, NB), bf16),
            pltpu.VMEM((NB, NB), f32),
            pltpu.VMEM((2, RB, 128), f32),
            pltpu.SemaphoreType.DMA((2, NSEM)),
            pltpu.SemaphoreType.DMA((2, NSEM)),
            pltpu.SemaphoreType.DMA((8,)),
            pltpu.SemaphoreType.DMA((5,)),
        ],
        compiler_params=pltpu.CompilerParams(
            collective_id=0, has_side_effects=True, vmem_limit_bytes=12 * MIB
        ),
        cost_estimate=pl.CostEstimate(flops=20 * 10**9, bytes_accessed=0, transcendentals=0),
        name="panel",
    )(*inputs)
    rowp = rowp.reshape(2, mr, 128)
    colp = colp.reshape(2, mc, 128)
    tm = 384
    whole = lambda shape: pl.BlockSpec(shape, lambda i: (0, 0))
    out, vec, panel, white = pl.pallas_call(
        update_kernel,
        grid=(mr // tm,),
        out_shape=(
            jax.ShapeDtypeStruct((mr, mc), bf16),
            jax.ShapeDtypeStruct((nv, mr), f32),
            jax.ShapeDtypeStruct((RB, NB), f32),
            jax.ShapeDtypeStruct((nv, NB), f32),
        ),
        in_specs=[VM] * 7,
        out_specs=(
            pl.BlockSpec((tm, mc), lambda i: (i, 0)),
            whole((nv, mr)),
            whole((RB, NB)),
            whole((nv, NB)),
        ),
        compiler_params=pltpu.CompilerParams(vmem_limit_bytes=40 * MIB),
        name="update",
    )(rowp, colp, tiles, wh, rest, panel, white)
    return (panel, out, white, vec)


def solution(mesh):
    in_specs = (P(), P(("row", "col"), None), P("row", "col"), P("col", None), P("col", "row"))
    out_specs = (P(("row", "col"), None), P("row", "col"), P("col", None), P("col", "row"))
    return jax.shard_map(per_device, mesh=mesh, in_specs=in_specs, out_specs=out_specs, check_vma=False)
```
